32 devices in a mesh: mom: 8 (over z, y), tm: 4 (over x, core).
Axes of the slice: x: 2, y: 2, z: 4, core: 2. Of those that a mesh axis runs over, the one named last changes fastest.
Arguments:
- history: float32 [4, 8, 640, 1024], P(None, 'mom', None, 'tm'), may hold values from -6 to 6
- sigma_first: float32 [4, 128, 1024], P(None, None, 'tm'), may hold values from -4 to 4
- propagator: float32 [4, 8, 384], P(None, 'mom'), may hold values from -4 to 4
Outputs:
- green_last: float32 [4, 8, 128, 1024], P(None, 'mom', None, 'tm')
- sigma_next: float32 [4, 128, 1024], P(None, None, 'tm')
The draws below stay inside these ranges and needn't reach their ends.
All inputs are finite; a program needn't handle non-finite values.
Results may differ from the reference program's by a relative error of at most 0.0003.
Values sent between devices are 32-bit elements; how exact they have to be, the bound alone decides.
A program may use at most 64 MiB of HBM per device.

```python
import jax
import jax.numpy as jnp
from jax import lax

NT = 1024
BLK = 128
NBLK = 3
MOMENTA = 8
HIST = 640
NEW = 384


def levels(key, shape, shards, smallest, top_value):
    def one(dim, blocks):
        draws = jax.random.uniform(jax.random.fold_in(jax.random.fold_in(key, 6), dim), (blocks,), jnp.float32, smallest / len(shards), top_value / len(shards))
        return jnp.repeat(jnp.exp(draws), shape[dim] // blocks).reshape((-1,) + (1,) * (len(shape) - dim - 1))

    gain = one(*shards[0])
    for cut in shards[1:]:
        gain = gain * one(*cut)
    return gain


def bell_draw(rng, extent, width, bound, pieces=(), kind=jnp.bfloat16):
    level = levels(rng, extent, pieces, -0.22, 0.18) if pieces else 1.0
    entries = jax.random.normal(rng, extent, jnp.float32) * width * level
    return jnp.minimum(jnp.maximum(entries, -bound), bound).astype(kind)


def setup_inputs(seed: int = 0) -> dict:
    keys = jax.random.split(jax.random.key(seed), 4)
    history = bell_draw(keys[0], (4, MOMENTA, HIST, NT), 1.0, 6.0, ((1, 8), (3, 4)), jnp.float32)
    sigma_first = bell_draw(keys[1], (4, BLK, NT), 0.3, 4.0, ((2, 4),), jnp.float32)
    propagator = bell_draw(keys[2], (4, MOMENTA, NEW), 0.6, 4.0, ((1, 8),), jnp.float32)
    return {"history": history, "sigma_first": sigma_first, "propagator": propagator}


def contract(sigma, rows):
    parts = []
    for orbital in range(2):
        s_re = sigma[2 * orbital]
        s_im = sigma[2 * orbital + 1]
        h_re = rows[2 * orbital]
        h_im = rows[2 * orbital + 1]
        hp = lax.Precision.HIGHEST
        real_part = jnp.einsum('tu,kus->kts', s_re, h_re, precision=hp) - jnp.einsum('tu,kus->kts', s_im, h_im, precision=hp)
        imag_part = jnp.einsum('tu,kus->kts', s_re, h_im, precision=hp) + jnp.einsum('tu,kus->kts', s_im, h_re, precision=hp)
        parts.append(real_part)
        parts.append(imag_part)
    return jnp.stack(parts)

def cubic(local):
    parts = []
    for orbital in range(2):
        a_part = local[2 * orbital]
        b_part = local[2 * orbital + 1]
        parts.append(0.1 * (a_part * a_part * a_part - 3.0 * a_part * b_part * b_part))
        parts.append(0.1 * (3.0 * a_part * a_part * b_part - b_part * b_part * b_part))
    return jnp.stack(parts)

def advance(previous, convolved, factor, row_ids, col_ids, step_size):
    inner = previous + step_size * convolved
    parts = []
    for orbital in range(2):
        p_re = factor[2 * orbital][:, :, None]
        p_im = factor[2 * orbital + 1][:, :, None]
        x_re = inner[2 * orbital]
        x_im = inner[2 * orbital + 1]
        parts.append(p_re * x_re - p_im * x_im)
        parts.append(p_re * x_im + p_im * x_re)
    keep = (col_ids[None, :] <= row_ids[:, None]).astype(jnp.float32)
    return jnp.stack(parts) * keep[None, None]

def reference(history, sigma_first, propagator):
    step_size = 1.0 / jnp.sqrt(jnp.float32(NT))
    col_ids = jnp.arange(NT, dtype=jnp.int32)
    hist_rows = jnp.arange(HIST, dtype=jnp.int32)
    known = history * (col_ids[None, :] <= hist_rows[:, None]).astype(jnp.float32)[None, None]
    window = jnp.zeros((4, MOMENTA, NEW, NT), jnp.float32)
    sigma = sigma_first
    green = None
    for block in range(NBLK):
        start = HIST + block * BLK
        convolved = contract(sigma[:, :, :HIST], known) + contract(sigma[:, :, HIST:], window)
        if block == 0:
            previous = known[:, :, HIST - BLK:HIST, :]
        else:
            previous = window[:, :, start - BLK - HIST:start - HIST, :]
        row_ids = start + jnp.arange(BLK, dtype=jnp.int32)
        factor = propagator[:, :, block * BLK:(block + 1) * BLK]
        green = advance(previous, convolved, factor, row_ids, col_ids, step_size)
        window = window.at[:, :, block * BLK:(block + 1) * BLK, :].set(green)
        local = lax.optimization_barrier(jnp.sum(green, axis=1)) / jnp.sqrt(jnp.float32(MOMENTA))
        sigma = cubic(local)
    return (green, sigma)
```

```python
import functools
import math

import jax
import jax.numpy as jnp
from jax import lax
from jax.experimental import pallas as pl
from jax.experimental.pallas import tpu as pltpu
from jax.sharding import PartitionSpec as P

MESH = pl.DeviceIdType.MESH
PAIR = 2
SUBLANES = 8


def contract(sigma, rows):
    parts = []
    for orbital in range(2):
        s_re = sigma[2 * orbital]
        s_im = sigma[2 * orbital + 1]
        h_re = rows[2 * orbital]
        h_im = rows[2 * orbital + 1]
        hp = lax.Precision.HIGHEST
        real_part = jnp.einsum("tu,kus->kts", s_re, h_re, precision=hp) - jnp.einsum(
            "tu,kus->kts", s_im, h_im, precision=hp
        )
        imag_part = jnp.einsum("tu,kus->kts", s_re, h_im, precision=hp) + jnp.einsum(
            "tu,kus->kts", s_im, h_re, precision=hp
        )
        parts.append(real_part)
        parts.append(imag_part)
    return jnp.stack(parts)


def cubic_pair(a_part, b_part):
    return (
        0.1 * (a_part * a_part * a_part - 3.0 * a_part * b_part * b_part),
        0.1 * (3.0 * a_part * a_part * b_part - b_part * b_part * b_part),
    )


def cubic(local):
    return jnp.stack(cubic_pair(local[0], local[1]) + cubic_pair(local[2], local[3]))


def advance(previous, convolved, factor, row_ids, col_ids, step_size):
    inner = previous + step_size * convolved
    parts = []
    for orbital in range(2):
        p_re = factor[2 * orbital][:, :, None]
        p_im = factor[2 * orbital + 1][:, :, None]
        x_re = inner[2 * orbital]
        x_im = inner[2 * orbital + 1]
        parts.append(p_re * x_re - p_im * x_im)
        parts.append(p_re * x_im + p_im * x_re)
    keep = (col_ids[None, :] <= row_ids[:, None]).astype(jnp.float32)
    return jnp.stack(parts) * keep[None, None]


def plain_body(history, sigma_first, propagator):
    local_moms = history.shape[1]
    hist_rows = history.shape[2]
    cols = history.shape[3]
    rows_block = sigma_first.shape[1]
    new_rows = propagator.shape[2]
    blocks = new_rows // rows_block
    time_shards = lax.axis_size("tm")
    mom_shards = lax.axis_size("mom")
    step_size = 1.0 / jnp.sqrt(jnp.float32(cols * time_shards))
    norm_factor = 1.0 / jnp.sqrt(jnp.float32(local_moms * mom_shards))
    col_ids = lax.axis_index("tm") * cols + jnp.arange(cols, dtype=jnp.int32)
    known_ids = jnp.arange(hist_rows, dtype=jnp.int32)
    known = history * (col_ids[None, :] <= known_ids[:, None]).astype(jnp.float32)[None, None]
    buffer = jnp.concatenate(
        [known, jnp.zeros((4, local_moms, new_rows, cols), jnp.float32)], axis=2
    )
    sigma_cols = sigma_first
    green = None
    for block in range(blocks):
        sigma_full = lax.all_gather(sigma_cols, "tm", axis=2, tiled=True)
        start = hist_rows + block * rows_block
        convolved = contract(sigma_full, buffer)
        previous = buffer[:, :, start - rows_block : start, :]
        row_ids = start + jnp.arange(rows_block, dtype=jnp.int32)
        factor = propagator[:, :, block * rows_block : (block + 1) * rows_block]
        green = advance(previous, convolved, factor, row_ids, col_ids, step_size)
        buffer = lax.dynamic_update_slice_in_dim(buffer, green, start, 2)
        local = lax.psum(jnp.sum(green, axis=1), "mom") * norm_factor
        sigma_cols = cubic(local)
    return (green, sigma_cols)


def split(x):
    high = x.astype(jnp.bfloat16)
    return high, (x - high.astype(jnp.float32)).astype(jnp.bfloat16)


def window_kernel(
    moms, shards,
    hist_ref, sig_ref, prop_ref, green_ref, next_ref,
    hist32, gh, gl, gcur, ybuf, part, zbuf, s32, conv,
    load_sem, ys, yr, zs, zr, gzs, gzr, gys, gyr, ts, tr,
):
    orbitals, _, hist_rows, cols = hist_ref.shape
    rows = sig_ref.shape[2]
    blocks = prop_ref.shape[0] // rows
    outer = moms // PAIR
    half = rows // PAIR
    piece = half // outer
    dt = 1.0 / math.sqrt(cols * shards)
    norm = 1.0 / math.sqrt(moms)
    mom = lax.axis_index("mom")
    tm = lax.axis_index("tm")
    y = lax.rem(mom, PAIR)
    z = lax.div(mom, PAIR)
    partner = z * PAIR + (1 - y)
    peers = [lax.rem(z + d, outer) * PAIR + y for d in range(1, outer)]

    loads = [pltpu.make_async_copy(sig_ref, s32.at[0, :, tm], load_sem.at[0])]
    loads += [
        pltpu.make_async_copy(hist_ref.at[o], hist32.at[o], load_sem.at[1 + o]) for o in range(orbitals)
    ]
    for load in loads:
        load.start()

    barrier = pltpu.get_barrier_semaphore()
    pl.semaphore_signal(barrier, inc=1, device_id=(partner, tm), device_id_type=MESH)
    for peer in peers:
        pl.semaphore_signal(barrier, inc=1, device_id=(peer, tm), device_id_type=MESH)
    for d in range(1, shards):
        pl.semaphore_signal(
            barrier, inc=1, device_id=(mom, lax.rem(tm + d, shards)), device_id_type=MESH
        )
    pl.semaphore_wait(barrier, 1 + len(peers) + shards - 1)

    def width(b, shard):
        return max(0, min(cols, hist_rows + b * rows - shard * cols))

    def share(b, o, src, dst):
        view = s32.at[b, o, src, :, :, pl.ds(0, width(b, src))]
        return pltpu.make_async_remote_copy(
            src_ref=view, dst_ref=view, send_sem=ts.at[b, o, dst], recv_sem=tr.at[b, o, src],
            device_id=(mom, jnp.int32(dst)), device_id_type=MESH,
        )

    def spread(b, o):
        for src in range(1, shards):
            if width(b, src):
                @pl.when(tm == src)
                def _():
                    for dst in range(src):
                        share(b, o, src, dst).start()

    half_mine = pl.ds(pl.multiple_of(y * half, half), half)
    half_other = pl.ds(pl.multiple_of((1 - y) * half, half), half)
    own = pl.ds(pl.multiple_of(y * half + z * piece, piece), piece)

    def pair_sum(b, o):
        return pltpu.make_async_remote_copy(
            src_ref=gcur.at[b, o, :, half_other], dst_ref=ybuf.at[b, o],
            send_sem=ys.at[b, o], recv_sem=yr.at[b, o],
            device_id=(partner, tm), device_id_type=MESH,
        )

    def line_sum(b, o, d):
        target = lax.rem(z + d, outer)
        return pltpu.make_async_remote_copy(
            src_ref=part.at[b, o, :, pl.ds(pl.multiple_of(target * piece, piece), piece)],
            dst_ref=zbuf.at[b, o, d - 1],
            send_sem=zs.at[b, o, d - 1], recv_sem=zr.at[b, o, d - 1],
            device_id=(peers[d - 1], tm), device_id_type=MESH,
        )

    def line_copy(b, o, d):
        view = s32.at[b + 1, o, tm, :, own]
        return pltpu.make_async_remote_copy(
            src_ref=view, dst_ref=view,
            send_sem=gzs.at[b, o, d - 1], recv_sem=gzr.at[b, o, d - 1],
            device_id=(peers[d - 1], tm), device_id_type=MESH,
        )

    def pair_copy(b, o):
        view = s32.at[b + 1, o, tm, :, half_mine]
        return pltpu.make_async_remote_copy(
            src_ref=view, dst_ref=view, send_sem=gys.at[b, o], recv_sem=gyr.at[b, o],
            device_id=(partner, tm), device_id_type=MESH,
        )

    loads[0].wait()
    for o in range(orbitals):
        spread(0, o)

    col_ids = tm * cols + lax.broadcasted_iota(jnp.int32, (rows, cols), 1)
    row_iota = lax.broadcasted_iota(jnp.int32, (rows, cols), 0)
    for o in range(orbitals):
        loads[1 + o].wait()
        for r in range(0, hist_rows, rows):
            for c in range(2):
                x = jnp.where(col_ids <= row_iota + r, hist32[o, c, r : r + rows], 0.0)
                high, low = split(x)
                gh[o, c, r : r + rows] = high
                gl[o, c, r : r + rows] = low

    for b in range(blocks):
        start = hist_rows + b * rows
        last = b + 1 == blocks
        keep = col_ids <= row_iota + start
        active = tm * cols < start + rows

        for o in range(orbitals):
            conv[o] = jnp.zeros((2, rows, cols), jnp.float32)
            for shard in range(shards):
                depth = width(b, shard)
                if not depth:
                    continue

                @pl.when(tm < shard)
                def _():
                    share(b, o, shard, 0).wait_recv()

                @pl.when(tm <= shard)
                def _():
                    re_high, re_low = split(s32[b, o, shard, 0, :, 0:depth])
                    im_high, im_low = split(s32[b, o, shard, 1, :, 0:depth])
                    lhs_high = jnp.concatenate([re_high, im_high], axis=0)
                    lhs_both = jnp.concatenate([re_high, im_high, re_low, im_low], axis=0)
                    u = shard * cols
                    totals = []
                    for c in range(2):
                        main = jnp.dot(
                            lhs_both, gh[o, c, u : u + depth], preferred_element_type=jnp.float32
                        )
                        rest = jnp.dot(
                            lhs_high, gl[o, c, u : u + depth], preferred_element_type=jnp.float32
                        )
                        totals.append(main[: 2 * rows] + (main[2 * rows :] + rest))
                    conv[o, 0] += totals[0][:rows] - totals[1][rows:]
                    conv[o, 1] += totals[1][:rows] + totals[0][rows:]

            p_re = prop_ref[b * rows : (b + 1) * rows, 2 * o : 2 * o + 1]
            p_im = prop_ref[b * rows : (b + 1) * rows, 2 * o + 1 : 2 * o + 2]
            if b == 0:
                before = hist_rows - rows
                seen = col_ids <= row_iota + before
                prev = [jnp.where(seen, hist32[o, c, before:hist_rows], 0.0) for c in range(2)]
            else:
                prev = [gcur[b - 1, o, c] for c in range(2)]
            x_re = prev[0] + dt * conv[o, 0]
            x_im = prev[1] + dt * conv[o, 1]
            new = [
                jnp.where(keep, p_re * x_re - p_im * x_im, 0.0),
                jnp.where(keep, p_re * x_im + p_im * x_re, 0.0),
            ]
            for c in range(2):
                gcur[b, o, c] = new[c]

            @pl.when(active)
            def _():
                pair_sum(b, o).start()

            for c in range(2):
                if last:
                    green_ref[o, c] = new[c]
                else:
                    high, low = split(new[c])
                    gh[o, c, start : start + rows] = high
                    gl[o, c, start : start + rows] = low

        @pl.when(active)
        def _():
            for o in range(orbitals):
                pair_sum(b, o).wait_recv()
                part[b, o] = gcur[b, o, :, half_mine] + ybuf[b, o]
                for d in range(1, outer):
                    line_sum(b, o, d).start()
            for o in range(orbitals):
                total = part[b, o, :, pl.ds(pl.multiple_of(z * piece, piece), piece)]
                for d in range(1, outer):
                    line_sum(b, o, d).wait_recv()
                    total = total + zbuf[b, o, d - 1]
                total = total * norm
                s_re, s_im = cubic_pair(total[0], total[1])
                s32[b + 1, o, tm, 0, own] = s_re
                s32[b + 1, o, tm, 1, own] = s_im
                for d in range(1, outer):
                    line_copy(b, o, d).start()
            for o in range(orbitals):
                for d in range(1, outer):
                    line_copy(b, o, d).wait_recv()
                pair_copy(b, o).start()
            for o in range(orbitals):
                pair_copy(b, o).wait_recv()
                if not last:
                    spread(b + 1, o)

    for o in range(orbitals):
        next_ref[o] = s32[blocks, o, tm]

    for b in range(blocks):
        for o in range(orbitals):
            for src in range(1, shards):
                if width(b, src):
                    @pl.when(tm == src)
                    def _():
                        for dst in range(src):
                            share(b, o, src, dst).wait_send()

        @pl.when(tm * cols < hist_rows + (b + 1) * rows)
        def _():
            for o in range(orbitals):
                pair_sum(b, o).wait_send()
                pair_copy(b, o).wait_send()
                for d in range(1, outer):
                    line_sum(b, o, d).wait_send()
                    line_copy(b, o, d).wait_send()


def kernel_body(moms, shards, history, sigma_first, propagator):
    comps, _, hist_rows, cols = history.shape
    rows = sigma_first.shape[1]
    new_rows = propagator.shape[2]
    blocks = new_rows // rows
    orbitals = comps // 2
    outer = moms // PAIR
    half = rows // PAIR
    piece = half // outer
    f32, bf16 = jnp.float32, jnp.bfloat16
    dma = pltpu.SemaphoreType.DMA
    vmem = pl.BlockSpec(memory_space=pltpu.VMEM)
    hbm = pl.BlockSpec(memory_space=pl.ANY)
    line = (blocks, orbitals, max(outer - 1, 1))
    green, sigma = pl.pallas_call(
        functools.partial(window_kernel, moms, shards),
        out_shape=(
            jax.ShapeDtypeStruct((orbitals, 2, rows, cols), f32),
            jax.ShapeDtypeStruct((orbitals, 2, rows, cols), f32),
        ),
        in_specs=[hbm, hbm, vmem],
        out_specs=(vmem, vmem),
        scratch_shapes=[
            pltpu.VMEM((orbitals, 2, hist_rows, cols), f32),
            pltpu.VMEM((orbitals, 2, hist_rows + new_rows, cols), bf16),
            pltpu.VMEM((orbitals, 2, hist_rows + new_rows, cols), bf16),
            pltpu.VMEM((blocks, orbitals, 2, rows, cols), f32),
            pltpu.VMEM((blocks, orbitals, 2, half, cols), f32),
            pltpu.VMEM((blocks, orbitals, 2, half, cols), f32),
            pltpu.VMEM(line + (2, piece, cols), f32),
            pltpu.VMEM((blocks + 1, orbitals, shards, 2, rows, cols), f32),
            pltpu.VMEM((orbitals, 2, rows, cols), f32),
            dma((1 + orbitals,)),
            dma((blocks, orbitals)), dma((blocks, orbitals)),
            dma(line), dma(line), dma(line), dma(line),
            dma((blocks, orbitals)), dma((blocks, orbitals)),
            dma((blocks, orbitals, shards)), dma((blocks, orbitals, shards)),
        ],
        compiler_params=pltpu.CompilerParams(
            collective_id=0, has_side_effects=True, vmem_limit_bytes=56 * 1024 * 1024
        ),
    )(
        history.reshape(orbitals, 2, hist_rows, cols),
        sigma_first.reshape(orbitals, 2, rows, cols),
        propagator.reshape(comps, new_rows).T,
    )
    return green.reshape(comps, 1, rows, cols), sigma.reshape(comps, rows, cols)


def body(history, sigma_first, propagator):
    moms, shards = lax.axis_size("mom"), lax.axis_size("tm")
    rows = sigma_first.shape[1]
    tiled = moms % PAIR == 0 and rows % (moms * SUBLANES) == 0
    whole = history.shape[2] + propagator.shape[2] == history.shape[3] * shards
    if history.shape[1] == 1 and tiled and whole:
        return kernel_body(moms, shards, history, sigma_first, propagator)
    return plain_body(history, sigma_first, propagator)


def solution(mesh):
    placed = (P(None, "mom", None, "tm"), P(None, None, "tm"), P(None, "mom", None))
    return jax.shard_map(
        body,
        mesh=mesh,
        in_specs=placed,
        out_specs=(P(None, "mom", None, "tm"), P(None, None, "tm")),
        check_vma=False,
    )
```

```python
import functools
import math

import jax
import jax.numpy as jnp
from jax import lax
from jax.experimental import pallas as pl
from jax.experimental.pallas import tpu as pltpu
from jax.sharding import PartitionSpec as P

MESH = pl.DeviceIdType.MESH
PAIR = 2
SUBLANES = 8
LANES = 128
CHUNKS = 2


def contract(sigma, rows):
    parts = []
    for orbital in range(2):
        s_re = sigma[2 * orbital]
        s_im = sigma[2 * orbital + 1]
        h_re = rows[2 * orbital]
        h_im = rows[2 * orbital + 1]
        hp = lax.Precision.HIGHEST
        real_part = jnp.einsum("tu,kus->kts", s_re, h_re, precision=hp) - jnp.einsum(
            "tu,kus->kts", s_im, h_im, precision=hp
        )
        imag_part = jnp.einsum("tu,kus->kts", s_re, h_im, precision=hp) + jnp.einsum(
            "tu,kus->kts", s_im, h_re, precision=hp
        )
        parts.append(real_part)
        parts.append(imag_part)
    return jnp.stack(parts)


def cubic_pair(a_part, b_part):
    return (
        0.1 * (a_part * a_part * a_part - 3.0 * a_part * b_part * b_part),
        0.1 * (3.0 * a_part * a_part * b_part - b_part * b_part * b_part),
    )


def cubic(local):
    return jnp.stack(cubic_pair(local[0], local[1]) + cubic_pair(local[2], local[3]))


def advance(previous, convolved, factor, row_ids, col_ids, step_size):
    inner = previous + step_size * convolved
    parts = []
    for orbital in range(2):
        p_re = factor[2 * orbital][:, :, None]
        p_im = factor[2 * orbital + 1][:, :, None]
        x_re = inner[2 * orbital]
        x_im = inner[2 * orbital + 1]
        parts.append(p_re * x_re - p_im * x_im)
        parts.append(p_re * x_im + p_im * x_re)
    keep = (col_ids[None, :] <= row_ids[:, None]).astype(jnp.float32)
    return jnp.stack(parts) * keep[None, None]


def plain_body(history, sigma_first, propagator):
    local_moms = history.shape[1]
    hist_rows = history.shape[2]
    cols = history.shape[3]
    rows_block = sigma_first.shape[1]
    new_rows = propagator.shape[2]
    blocks = new_rows // rows_block
    time_shards = lax.axis_size("tm")
    mom_shards = lax.axis_size("mom")
    step_size = 1.0 / jnp.sqrt(jnp.float32(cols * time_shards))
    norm_factor = 1.0 / jnp.sqrt(jnp.float32(local_moms * mom_shards))
    col_ids = lax.axis_index("tm") * cols + jnp.arange(cols, dtype=jnp.int32)
    known_ids = jnp.arange(hist_rows, dtype=jnp.int32)
    known = history * (col_ids[None, :] <= known_ids[:, None]).astype(jnp.float32)[None, None]
    buffer = jnp.concatenate(
        [known, jnp.zeros((4, local_moms, new_rows, cols), jnp.float32)], axis=2
    )
    sigma_cols = sigma_first
    green = None
    for block in range(blocks):
        sigma_full = lax.all_gather(sigma_cols, "tm", axis=2, tiled=True)
        start = hist_rows + block * rows_block
        convolved = contract(sigma_full, buffer)
        previous = buffer[:, :, start - rows_block : start, :]
        row_ids = start + jnp.arange(rows_block, dtype=jnp.int32)
        factor = propagator[:, :, block * rows_block : (block + 1) * rows_block]
        green = advance(previous, convolved, factor, row_ids, col_ids, step_size)
        buffer = lax.dynamic_update_slice_in_dim(buffer, green, start, 2)
        local = lax.psum(jnp.sum(green, axis=1), "mom") * norm_factor
        sigma_cols = cubic(local)
    return (green, sigma_cols)


def split(x):
    high = x.astype(jnp.bfloat16)
    return high, (x - high.astype(jnp.float32)).astype(jnp.bfloat16)


def stage_order(blocks, tasks, last_stage):
    lag = (3.0, 4.0, 4.0, 3.0, 3.0, 1.5)
    busy = (1.0, 0.2, 0.2, 0.1, 0.1, 0.1)
    ready = [(0.0, 0, task, 0) for task in range(tasks)]
    now, order = 0.0, []
    while ready:
        item = min(ready)
        ready.remove(item)
        when, block, task, stage = item
        order.append((stage, block, task))
        now = max(now, when) + busy[stage]
        done = now + lag[stage]
        final = block + 1 == blocks
        if stage < last_stage and not (final and stage == 4):
            ready.append((done, block, task, stage + 1))
        elif not final:
            ready.append((done, block + 1, task, 0))
    return order


def window_kernel(
    moms, shards, chunks,
    hist_ref, sig_ref, prop_ref, green_ref, next_ref,
    hist32, gh, gl, gcur, ybuf, part, zbuf, s32, conv, pcol,
    load_sem, ys, yr, zs, zr, gzs, gzr, gys, gyr, ts, tr, fs, fr,
):
    orbitals, _, hist_rows, cols = hist_ref.shape
    rows = sig_ref.shape[2]
    blocks = prop_ref.shape[1] // rows
    outer = moms // PAIR
    w = rows // chunks
    half = cols // PAIR
    piece = w // outer
    dt = 1.0 / math.sqrt(cols * shards)
    norm = 1.0 / math.sqrt(moms)
    mom = lax.axis_index("mom")
    tm = lax.axis_index("tm")
    y = lax.rem(mom, PAIR)
    z = lax.div(mom, PAIR)
    partner = z * PAIR + (1 - y)
    peers = [lax.rem(z + d, outer) * PAIR + y for d in range(1, outer)]
    place = lax.rem(tm, PAIR)
    twin = tm + 1 - 2 * place

    loads = [pltpu.make_async_copy(sig_ref, s32.at[0, :, tm], load_sem.at[0])]
    loads += [
        pltpu.make_async_copy(hist_ref.at[o], hist32.at[o], load_sem.at[1 + o]) for o in range(orbitals)
    ]
    for load in loads:
        load.start()

    barrier = pltpu.get_barrier_semaphore()
    pl.semaphore_signal(barrier, inc=1, device_id=(partner, tm), device_id_type=MESH)
    for peer in peers:
        pl.semaphore_signal(barrier, inc=1, device_id=(peer, tm), device_id_type=MESH)
    for d in range(1, shards):
        pl.semaphore_signal(
            barrier, inc=1, device_id=(mom, lax.rem(tm + d, shards)), device_id_type=MESH
        )
    pl.semaphore_wait(barrier, 1 + len(peers) + shards - 1)

    def width(b, shard):
        return max(0, min(cols, hist_rows + b * rows - shard * cols))

    def remote(src, dst, send, recv, device):
        return pltpu.make_async_remote_copy(
            src_ref=src, dst_ref=dst, send_sem=send, recv_sem=recv,
            device_id=device, device_id_type=MESH,
        )

    def chunk(r):
        return pl.ds(r * w, w)

    def near(b, r, o, src):
        view = s32.at[b, o, src, :, chunk(r), pl.ds(0, width(b, src))]
        return remote(view, view, ts.at[b, r, o, 0], tr.at[b, r, o, src], (mom, jnp.int32(src - 1)))

    def far(b, r, o, src, dst):
        view = s32.at[b, o, src, dst % PAIR, chunk(r), pl.ds(0, width(b, src))]
        return remote(view, view, ts.at[b, r, o, 1 + dst], tr.at[b, r, o, src], (mom, jnp.int32(dst)))

    def passed(b, r, o, src, component):
        view = s32.at[b, o, src, component, chunk(r), pl.ds(0, width(b, src))]
        return remote(view, view, fs.at[b, r, o, src], fr.at[b, r, o, src], (mom, twin))

    def spread(b, r, o, act):
        for src in range(1, shards):
            base = src - src % PAIR
            if width(b, src):
                @pl.when(tm == src)
                def _():
                    for dst in range(base):
                        act(far(b, r, o, src, dst))
                    if src % PAIR:
                        act(near(b, r, o, src))

    def forward(b, r, o, go):
        for src in range(PAIR, shards):
            base = src - src % PAIR
            if width(b, src):
                @pl.when(tm < base)
                def _():
                    if go:
                        far(b, r, o, src, 0).wait_recv()
                        passed(b, r, o, src, place).start()
                    else:
                        passed(b, r, o, src, place).wait_send()

    half_mine = pl.ds(pl.multiple_of(y * half, LANES), half)
    half_other = pl.ds(pl.multiple_of((1 - y) * half, LANES), half)

    def strip(r, k):
        return pl.ds(pl.multiple_of(r * w + k * piece, SUBLANES), piece)

    def pair_sum(b, r, o):
        return remote(
            gcur.at[b, o, :, chunk(r), half_other], ybuf.at[b, r, o],
            ys.at[b, r, o], yr.at[b, r, o], (partner, tm),
        )

    def line_sum(b, r, o, d):
        target = lax.rem(z + d, outer)
        return remote(
            part.at[b, o, :, strip(r, target)], zbuf.at[b, r, o, d - 1],
            zs.at[b, r, o, d - 1], zr.at[b, r, o, d - 1], (peers[d - 1], tm),
        )

    def line_copy(b, r, o, d):
        view = s32.at[b + 1, o, tm, :, strip(r, z), half_mine]
        return remote(view, view, gzs.at[b, r, o, d - 1], gzr.at[b, r, o, d - 1], (peers[d - 1], tm))

    def pair_copy(b, r, o):
        view = s32.at[b + 1, o, tm, :, chunk(r), half_mine]
        return remote(view, view, gys.at[b, r, o], gyr.at[b, r, o], (partner, tm))

    tasks = [(r, o) for r in range(chunks) for o in range(orbitals)]
    start_copy = lambda copy: copy.start()
    loads[0].wait()
    for r, o in tasks:
        spread(0, r, o, start_copy)

    col_ids = tm * cols + lax.broadcasted_iota(jnp.int32, (rows, cols), 1)
    row_iota = lax.broadcasted_iota(jnp.int32, (rows, cols), 0)
    keep_cols = tm * cols + lax.broadcasted_iota(jnp.int32, (w, cols), 1)
    keep_rows = lax.broadcasted_iota(jnp.int32, (w, cols), 0)
    square = lax.broadcasted_iota(jnp.int32, (rows, rows), 0)
    diagonal = square == lax.broadcasted_iota(jnp.int32, (rows, rows), 1)
    for b in range(blocks):
        for c in range(2 * orbitals):
            line = prop_ref[c : c + 1, b * rows : (b + 1) * rows]
            pcol[b, c] = jnp.sum(jnp.where(diagonal, line, 0.0), axis=1, keepdims=True)
    gh[:, :, hist_rows:] = jnp.zeros((orbitals, 2, blocks * rows, cols), jnp.bfloat16)
    gl[:, :, hist_rows:] = jnp.zeros((orbitals, 2, blocks * rows, cols), jnp.bfloat16)
    for o in range(orbitals):
        loads[1 + o].wait()
        for r in range(0, hist_rows, rows):
            for c in range(2):
                x = jnp.where(col_ids <= row_iota + r, hist32[o, c, r : r + rows], 0.0)
                high, low = split(x)
                gh[o, c, r : r + rows] = high
                gl[o, c, r : r + rows] = low
    for r, o in tasks:
        forward(0, r, o, True)

    def compute(b, r, o):
        start = hist_rows + b * rows + r * w
        span = slice(r * w, (r + 1) * w)
        conv[...] = jnp.zeros(conv.shape, jnp.float32)
        for shard in range(shards):
            depth = width(b, shard)
            if not depth:
                continue
            base = shard - shard % PAIR
            if shard % PAIR:
                @pl.when(tm == base)
                def _():
                    near(b, r, o, shard).wait_recv()
            if base:
                @pl.when(tm < base)
                def _():
                    passed(b, r, o, shard, 0).wait_recv()

            @pl.when(tm <= shard)
            def _():
                re_high, re_low = split(s32[b, o, shard, 0, span, 0:depth])
                im_high, im_low = split(s32[b, o, shard, 1, span, 0:depth])
                lhs_high = jnp.concatenate([re_high, im_high], axis=0)
                lhs_both = jnp.concatenate([re_high, im_high, re_low, im_low], axis=0)
                u = shard * cols
                totals = []
                for c in range(2):
                    main = jnp.dot(
                        lhs_both, gh[o, c, u : u + depth], preferred_element_type=jnp.float32
                    )
                    rest = jnp.dot(
                        lhs_high, gl[o, c, u : u + depth], preferred_element_type=jnp.float32
                    )
                    totals.append(main[: 2 * w] + (main[2 * w :] + rest))
                conv[0] += totals[0][:w] - totals[1][w:]
                conv[1] += totals[1][:w] + totals[0][w:]

        p_re = pcol[b, 2 * o, span]
        p_im = pcol[b, 2 * o + 1, span]
        if b == 0:
            before = start - rows
            seen = keep_cols <= keep_rows + before
            prev = [jnp.where(seen, hist32[o, c, before : before + w], 0.0) for c in range(2)]
        else:
            prev = [gcur[b - 1, o, c, span] for c in range(2)]
        x_re = prev[0] + dt * conv[0]
        x_im = prev[1] + dt * conv[1]
        keep = keep_cols <= keep_rows + start
        new = [
            jnp.where(keep, p_re * x_re - p_im * x_im, 0.0),
            jnp.where(keep, p_re * x_im + p_im * x_re, 0.0),
        ]
        for c in range(2):
            gcur[b, o, c, span] = new[c]

        @pl.when(active(b))
        def _():
            pair_sum(b, r, o).start()

        for c in range(2):
            if b + 1 == blocks:
                green_ref[o, c, span] = new[c]
            else:
                high, low = split(new[c])
                gh[o, c, start : start + w] = high
                gl[o, c, start : start + w] = low

    def active(b):
        return tm * cols < hist_rows + (b + 1) * rows

    def sum_pair(b, r, o):
        pair_sum(b, r, o).wait_recv()
        part[b, o, :, chunk(r)] = gcur[b, o, :, chunk(r), half_mine] + ybuf[b, r, o]
        for d in range(1, outer):
            line_sum(b, r, o, d).start()

    def sum_line(b, r, o):
        total = part[b, o, :, strip(r, z)]
        for d in range(1, outer):
            line_sum(b, r, o, d).wait_recv()
            total = total + zbuf[b, r, o, d - 1]
        total = total * norm
        s_re, s_im = cubic_pair(total[0], total[1])
        s32[b + 1, o, tm, 0, strip(r, z), half_mine] = s_re
        s32[b + 1, o, tm, 1, strip(r, z), half_mine] = s_im
        for d in range(1, outer):
            line_copy(b, r, o, d).start()

    def copy_line(b, r, o):
        for d in range(1, outer):
            line_copy(b, r, o, d).wait_recv()
        pair_copy(b, r, o).start()

    def copy_pair(b, r, o):
        pair_copy(b, r, o).wait_recv()
        if b + 1 == blocks:
            next_ref[o, :, chunk(r)] = s32[blocks, o, tm, :, chunk(r)]
        else:
            spread(b + 1, r, o, start_copy)

    stages = (compute, sum_pair, sum_line, copy_line, copy_pair)
    for stage, b, task in stage_order(blocks, len(tasks), 5):
        r, o = tasks[task]
        if stage == 0:
            compute(b, r, o)
        elif stage == 5:
            forward(b + 1, r, o, True)
        else:
            @pl.when(active(b))
            def _():
                stages[stage](b, r, o)

    for b in range(blocks):
        for r, o in tasks:
            spread(b, r, o, lambda copy: copy.wait_send())
            forward(b, r, o, False)

            @pl.when(active(b))
            def _():
                pair_sum(b, r, o).wait_send()
                pair_copy(b, r, o).wait_send()
                for d in range(1, outer):
                    line_sum(b, r, o, d).wait_send()
                    line_copy(b, r, o, d).wait_send()


def kernel_body(moms, shards, history, sigma_first, propagator):
    comps, _, hist_rows, cols = history.shape
    rows = sigma_first.shape[1]
    new_rows = propagator.shape[2]
    blocks = new_rows // rows
    orbitals = comps // 2
    outer = moms // PAIR
    w = rows // CHUNKS
    half = cols // PAIR
    piece = w // outer
    f32, bf16 = jnp.float32, jnp.bfloat16
    dma = pltpu.SemaphoreType.DMA
    vmem = pl.BlockSpec(memory_space=pltpu.VMEM)
    hbm = pl.BlockSpec(memory_space=pl.ANY)
    task = (blocks, CHUNKS, orbitals)
    line = task + (max(outer - 1, 1),)
    green, sigma = pl.pallas_call(
        functools.partial(window_kernel, moms, shards, CHUNKS),
        out_shape=(
            jax.ShapeDtypeStruct((orbitals, 2, rows, cols), f32),
            jax.ShapeDtypeStruct((orbitals, 2, rows, cols), f32),
        ),
        in_specs=[hbm, hbm, vmem],
        out_specs=(vmem, vmem),
        scratch_shapes=[
            pltpu.VMEM((orbitals, 2, hist_rows, cols), f32),
            pltpu.VMEM((orbitals, 2, hist_rows + new_rows, cols), bf16),
            pltpu.VMEM((orbitals, 2, hist_rows + new_rows, cols), bf16),
            pltpu.VMEM((blocks, orbitals, 2, rows, cols), f32),
            pltpu.VMEM(task + (2, w, half), f32),
            pltpu.VMEM((blocks, orbitals, 2, rows, half), f32),
            pltpu.VMEM(line + (2, piece, half), f32),
            pltpu.VMEM((blocks + 1, orbitals, shards, 2, rows, cols), f32),
            pltpu.VMEM((2, w, cols), f32),
            pltpu.VMEM((blocks, comps, rows, 1), f32),
            dma((1 + orbitals,)),
            dma(task), dma(task),
            dma(line), dma(line), dma(line), dma(line),
            dma(task), dma(task),
            dma(task + (shards,)), dma(task + (shards,)),
            dma(task + (shards,)), dma(task + (shards,)),
        ],
        compiler_params=pltpu.CompilerParams(
            collective_id=0, has_side_effects=True, vmem_limit_bytes=56 * 1024 * 1024
        ),
    )(
        history.reshape(orbitals, 2, hist_rows, cols),
        sigma_first.reshape(orbitals, 2, rows, cols),
        propagator.reshape(comps, new_rows),
    )
    return green.reshape(comps, 1, rows, cols), sigma.reshape(comps, rows, cols)


def body(history, sigma_first, propagator):
    moms, shards = lax.axis_size("mom"), lax.axis_size("tm")
    rows = sigma_first.shape[1]
    tiled = moms % PAIR == 0 and rows % (CHUNKS * (moms // PAIR) * SUBLANES) == 0
    tiled = tiled and shards % PAIR == 0 and history.shape[3] % (PAIR * LANES) == 0
    tiled = tiled and rows % LANES == 0 and history.shape[2] % LANES == 0
    whole = history.shape[2] + propagator.shape[2] == history.shape[3] * shards
    if history.shape[1] == 1 and tiled and whole:
        return kernel_body(moms, shards, history, sigma_first, propagator)
    return plain_body(history, sigma_first, propagator)


def solution(mesh):
    placed = (P(None, "mom", None, "tm"), P(None, None, "tm"), P(None, "mom", None))
    return jax.shard_map(
        body,
        mesh=mesh,
        in_specs=placed,
        out_specs=(P(None, "mom", None, "tm"), P(None, None, "tm")),
        check_vma=False,
    )
```

```python
import functools
import math

import jax
import jax.numpy as jnp
from jax import lax
from jax.experimental import pallas as pl
from jax.experimental.pallas import tpu as pltpu
from jax.sharding import PartitionSpec as P

MESH = pl.DeviceIdType.MESH
PAIR = 2
SUBLANES = 8
LANES = 128
CHUNKS = 2


def contract(sigma, rows):
    parts = []
    for orbital in range(2):
        s_re = sigma[2 * orbital]
        s_im = sigma[2 * orbital + 1]
        h_re = rows[2 * orbital]
        h_im = rows[2 * orbital + 1]
        hp = lax.Precision.HIGHEST
        real_part = jnp.einsum("tu,kus->kts", s_re, h_re, precision=hp) - jnp.einsum(
            "tu,kus->kts", s_im, h_im, precision=hp
        )
        imag_part = jnp.einsum("tu,kus->kts", s_re, h_im, precision=hp) + jnp.einsum(
            "tu,kus->kts", s_im, h_re, precision=hp
        )
        parts.append(real_part)
        parts.append(imag_part)
    return jnp.stack(parts)


def cubic_pair(a_part, b_part):
    return (
        0.1 * (a_part * a_part * a_part - 3.0 * a_part * b_part * b_part),
        0.1 * (3.0 * a_part * a_part * b_part - b_part * b_part * b_part),
    )


def cubic(local):
    return jnp.stack(cubic_pair(local[0], local[1]) + cubic_pair(local[2], local[3]))


def advance(previous, convolved, factor, row_ids, col_ids, step_size):
    inner = previous + step_size * convolved
    parts = []
    for orbital in range(2):
        p_re = factor[2 * orbital][:, :, None]
        p_im = factor[2 * orbital + 1][:, :, None]
        x_re = inner[2 * orbital]
        x_im = inner[2 * orbital + 1]
        parts.append(p_re * x_re - p_im * x_im)
        parts.append(p_re * x_im + p_im * x_re)
    keep = (col_ids[None, :] <= row_ids[:, None]).astype(jnp.float32)
    return jnp.stack(parts) * keep[None, None]


def plain_body(history, sigma_first, propagator):
    local_moms = history.shape[1]
    hist_rows = history.shape[2]
    cols = history.shape[3]
    rows_block = sigma_first.shape[1]
    new_rows = propagator.shape[2]
    blocks = new_rows // rows_block
    time_shards = lax.axis_size("tm")
    mom_shards = lax.axis_size("mom")
    step_size = 1.0 / jnp.sqrt(jnp.float32(cols * time_shards))
    norm_factor = 1.0 / jnp.sqrt(jnp.float32(local_moms * mom_shards))
    col_ids = lax.axis_index("tm") * cols + jnp.arange(cols, dtype=jnp.int32)
    known_ids = jnp.arange(hist_rows, dtype=jnp.int32)
    known = history * (col_ids[None, :] <= known_ids[:, None]).astype(jnp.float32)[None, None]
    buffer = jnp.concatenate(
        [known, jnp.zeros((4, local_moms, new_rows, cols), jnp.float32)], axis=2
    )
    sigma_cols = sigma_first
    green = None
    for block in range(blocks):
        sigma_full = lax.all_gather(sigma_cols, "tm", axis=2, tiled=True)
        start = hist_rows + block * rows_block
        convolved = contract(sigma_full, buffer)
        previous = buffer[:, :, start - rows_block : start, :]
        row_ids = start + jnp.arange(rows_block, dtype=jnp.int32)
        factor = propagator[:, :, block * rows_block : (block + 1) * rows_block]
        green = advance(previous, convolved, factor, row_ids, col_ids, step_size)
        buffer = lax.dynamic_update_slice_in_dim(buffer, green, start, 2)
        local = lax.psum(jnp.sum(green, axis=1), "mom") * norm_factor
        sigma_cols = cubic(local)
    return (green, sigma_cols)


def split(x):
    high = x.astype(jnp.bfloat16)
    return high, (x - high.astype(jnp.float32)).astype(jnp.bfloat16)


def stage_order(blocks, tasks, last_stage):
    lag = (3.0, 4.0, 4.0, 3.0, 3.0, 1.5)
    busy = (1.0, 0.2, 0.2, 0.1, 0.1, 0.1)
    ready = [(0.0, 0, task, 0) for task in range(tasks)]
    now, order = 0.0, []
    while ready:
        item = min(ready)
        ready.remove(item)
        when, block, task, stage = item
        order.append((stage, block, task))
        now = max(now, when) + busy[stage]
        done = now + lag[stage]
        final = block + 1 == blocks
        if stage < last_stage and not (final and stage == 4):
            ready.append((done, block, task, stage + 1))
        elif not final:
            ready.append((done, block + 1, task, 0))
    return order


def window_kernel(
    moms, shards, chunks,
    hist_ref, sig_ref, prop_ref, green_ref, next_ref,
    hist32, gh, gl, gcur, ybuf, part, zbuf, s32, conv, pcol,
    load_sem, ys, yr, zs, zr, gzs, gzr, gys, gyr, ts, tr, fs, fr,
):
    orbitals, _, hist_rows, cols = hist_ref.shape
    rows = sig_ref.shape[2]
    blocks = prop_ref.shape[2] // rows
    outer = moms // PAIR
    w = rows // chunks
    half = cols // PAIR
    piece = w // outer
    dt = 1.0 / math.sqrt(cols * shards)
    norm = 1.0 / math.sqrt(moms)
    mom = lax.axis_index("mom")
    tm = lax.axis_index("tm")
    y = lax.rem(mom, PAIR)
    z = lax.div(mom, PAIR)
    partner = z * PAIR + (1 - y)
    peers = [lax.rem(z + d, outer) * PAIR + y for d in range(1, outer)]
    place = lax.rem(tm, PAIR)
    twin = tm + 1 - 2 * place

    loads = [pltpu.make_async_copy(sig_ref, s32.at[0, :, tm], load_sem.at[0])]
    loads += [
        pltpu.make_async_copy(hist_ref.at[o], hist32.at[o], load_sem.at[1 + o]) for o in range(orbitals)
    ]
    for load in loads:
        load.start()

    barrier = pltpu.get_barrier_semaphore()
    pl.semaphore_signal(barrier, inc=1, device_id=(partner, tm), device_id_type=MESH)
    for peer in peers:
        pl.semaphore_signal(barrier, inc=1, device_id=(peer, tm), device_id_type=MESH)
    for d in range(1, shards):
        pl.semaphore_signal(
            barrier, inc=1, device_id=(mom, lax.rem(tm + d, shards)), device_id_type=MESH
        )
    pl.semaphore_wait(barrier, 1 + len(peers) + shards - 1)

    def width(b, shard):
        return max(0, min(cols, hist_rows + b * rows - shard * cols))

    def remote(src, dst, send, recv, device):
        return pltpu.make_async_remote_copy(
            src_ref=src, dst_ref=dst, send_sem=send, recv_sem=recv,
            device_id=device, device_id_type=MESH,
        )

    def chunk(r):
        return pl.ds(r * w, w)

    def near(b, r, o, src):
        view = s32.at[b, o, src, :, chunk(r), pl.ds(0, width(b, src))]
        return remote(view, view, ts.at[b, r, o, 0], tr.at[b, r, o, src], (mom, jnp.int32(src - 1)))

    def far(b, r, o, src, dst):
        view = s32.at[b, o, src, dst % PAIR, chunk(r), pl.ds(0, width(b, src))]
        return remote(view, view, ts.at[b, r, o, 1 + dst], tr.at[b, r, o, src], (mom, jnp.int32(dst)))

    def passed(b, r, o, src, component):
        view = s32.at[b, o, src, component, chunk(r), pl.ds(0, width(b, src))]
        return remote(view, view, fs.at[b, r, o, src], fr.at[b, r, o, src], (mom, twin))

    def spread(b, r, o, act):
        for src in range(1, shards):
            base = src - src % PAIR
            if width(b, src):
                @pl.when(tm == src)
                def _():
                    for dst in range(base):
                        act(far(b, r, o, src, dst))
                    if src % PAIR:
                        act(near(b, r, o, src))

    def forward(b, r, o, go):
        for src in range(PAIR, shards):
            base = src - src % PAIR
            if width(b, src):
                @pl.when(tm < base)
                def _():
                    if go:
                        far(b, r, o, src, 0).wait_recv()
                        passed(b, r, o, src, place).start()
                    else:
                        passed(b, r, o, src, place).wait_send()

    half_mine = pl.ds(pl.multiple_of(y * half, LANES), half)
    half_other = pl.ds(pl.multiple_of((1 - y) * half, LANES), half)

    def strip(r, k):
        return pl.ds(pl.multiple_of(r * w + k * piece, SUBLANES), piece)

    def pair_sum(b, r, o):
        return remote(
            gcur.at[b, o, :, chunk(r), half_other], ybuf.at[b, r, o],
            ys.at[b, r, o], yr.at[b, r, o], (partner, tm),
        )

    def line_sum(b, r, o, d):
        target = lax.rem(z + d, outer)
        return remote(
            part.at[b, o, :, strip(r, target)], zbuf.at[b, r, o, d - 1],
            zs.at[b, r, o, d - 1], zr.at[b, r, o, d - 1], (peers[d - 1], tm),
        )

    def line_copy(b, r, o, d):
        view = s32.at[b + 1, o, tm, :, strip(r, z), half_mine]
        return remote(view, view, gzs.at[b, r, o, d - 1], gzr.at[b, r, o, d - 1], (peers[d - 1], tm))

    def pair_copy(b, r, o):
        view = s32.at[b + 1, o, tm, :, chunk(r), half_mine]
        return remote(view, view, gys.at[b, r, o], gyr.at[b, r, o], (partner, tm))

    tasks = [(r, o) for r in range(chunks) for o in range(orbitals)]
    start_copy = lambda copy: copy.start()
    loads[0].wait()
    for r, o in tasks:
        spread(0, r, o, start_copy)

    col_ids = tm * cols + lax.broadcasted_iota(jnp.int32, (rows, cols), 1)
    row_iota = lax.broadcasted_iota(jnp.int32, (rows, cols), 0)
    keep_cols = tm * cols + lax.broadcasted_iota(jnp.int32, (w, cols), 1)
    keep_rows = lax.broadcasted_iota(jnp.int32, (w, cols), 0)
    square = lax.broadcasted_iota(jnp.int32, (rows, rows), 0)
    diagonal = square == lax.broadcasted_iota(jnp.int32, (rows, rows), 1)
    for b in range(blocks):
        for c in range(2 * orbitals):
            line = prop_ref[c, :, b * rows : (b + 1) * rows]
            pcol[b, c] = jnp.sum(jnp.where(diagonal, line, 0.0), axis=1, keepdims=True)
    gh[:, :, hist_rows:] = jnp.zeros((orbitals, 2, blocks * rows, cols), jnp.bfloat16)
    gl[:, :, hist_rows:] = jnp.zeros((orbitals, 2, blocks * rows, cols), jnp.bfloat16)
    for o in range(orbitals):
        loads[1 + o].wait()
        for r in range(0, hist_rows, rows):
            for c in range(2):
                x = jnp.where(col_ids <= row_iota + r, hist32[o, c, r : r + rows], 0.0)
                high, low = split(x)
                gh[o, c, r : r + rows] = high
                gl[o, c, r : r + rows] = low
    for r, o in tasks:
        forward(0, r, o, True)

    def compute(b, r, o):
        start = hist_rows + b * rows + r * w
        span = slice(r * w, (r + 1) * w)
        conv[...] = jnp.zeros(conv.shape, jnp.float32)
        for shard in range(shards):
            depth = width(b, shard)
            if not depth:
                continue
            base = shard - shard % PAIR
            if shard % PAIR:
                @pl.when(tm == base)
                def _():
                    near(b, r, o, shard).wait_recv()
            if base:
                @pl.when(tm < base)
                def _():
                    passed(b, r, o, shard, 0).wait_recv()

            @pl.when(tm <= shard)
            def _():
                re_high, re_low = split(s32[b, o, shard, 0, span, 0:depth])
                im_high, im_low = split(s32[b, o, shard, 1, span, 0:depth])
                lhs_high = jnp.concatenate([re_high, im_high], axis=0)
                lhs_both = jnp.concatenate([re_high, im_high, re_low, im_low], axis=0)
                u = shard * cols
                totals = []
                for c in range(2):
                    main = jnp.dot(
                        lhs_both, gh[o, c, u : u + depth], preferred_element_type=jnp.float32
                    )
                    rest = jnp.dot(
                        lhs_high, gl[o, c, u : u + depth], preferred_element_type=jnp.float32
                    )
                    totals.append(main[: 2 * w] + (main[2 * w :] + rest))
                conv[0] += totals[0][:w] - totals[1][w:]
                conv[1] += totals[1][:w] + totals[0][w:]

        p_re = pcol[b, 2 * o, span]
        p_im = pcol[b, 2 * o + 1, span]
        if b == 0:
            before = start - rows
            seen = keep_cols <= keep_rows + before
            prev = [jnp.where(seen, hist32[o, c, before : before + w], 0.0) for c in range(2)]
        else:
            prev = [gcur[b - 1, o, c, span] for c in range(2)]
        x_re = prev[0] + dt * conv[0]
        x_im = prev[1] + dt * conv[1]
        keep = keep_cols <= keep_rows + start
        new = [
            jnp.where(keep, p_re * x_re - p_im * x_im, 0.0),
            jnp.where(keep, p_re * x_im + p_im * x_re, 0.0),
        ]
        for c in range(2):
            gcur[b, o, c, span] = new[c]

        @pl.when(active(b))
        def _():
            pair_sum(b, r, o).start()

        for c in range(2):
            if b + 1 == blocks:
                green_ref[o, c, span] = new[c]
            else:
                high, low = split(new[c])
                gh[o, c, start : start + w] = high
                gl[o, c, start : start + w] = low

    def active(b):
        return tm * cols < hist_rows + (b + 1) * rows

    def sum_pair(b, r, o):
        pair_sum(b, r, o).wait_recv()
        part[b, o, :, chunk(r)] = gcur[b, o, :, chunk(r), half_mine] + ybuf[b, r, o]
        for d in range(1, outer):
            line_sum(b, r, o, d).start()

    def sum_line(b, r, o):
        total = part[b, o, :, strip(r, z)]
        for d in range(1, outer):
            line_sum(b, r, o, d).wait_recv()
            total = total + zbuf[b, r, o, d - 1]
        total = total * norm
        s_re, s_im = cubic_pair(total[0], total[1])
        s32[b + 1, o, tm, 0, strip(r, z), half_mine] = s_re
        s32[b + 1, o, tm, 1, strip(r, z), half_mine] = s_im
        for d in range(1, outer):
            line_copy(b, r, o, d).start()

    def copy_line(b, r, o):
        for d in range(1, outer):
            line_copy(b, r, o, d).wait_recv()
        pair_copy(b, r, o).start()

    def copy_pair(b, r, o):
        pair_copy(b, r, o).wait_recv()
        if b + 1 == blocks:
            next_ref[o, :, chunk(r)] = s32[blocks, o, tm, :, chunk(r)]
        else:
            spread(b + 1, r, o, start_copy)

    stages = (compute, sum_pair, sum_line, copy_line, copy_pair)
    for stage, b, task in stage_order(blocks, len(tasks), 5):
        r, o = tasks[task]
        if stage == 0:
            compute(b, r, o)
        elif stage == 5:
            forward(b + 1, r, o, True)
        else:
            @pl.when(active(b))
            def _():
                stages[stage](b, r, o)

    for b in range(blocks):
        for r, o in tasks:
            spread(b, r, o, lambda copy: copy.wait_send())
            forward(b, r, o, False)

            @pl.when(active(b))
            def _():
                pair_sum(b, r, o).wait_send()
                pair_copy(b, r, o).wait_send()
                for d in range(1, outer):
                    line_sum(b, r, o, d).wait_send()
                    line_copy(b, r, o, d).wait_send()


def deliver(green_ref, sigma_ref, green_out, sigma_out):
    green_out[...] = green_ref[...]
    sigma_out[...] = sigma_ref[...]


def kernel_body(moms, shards, history, sigma_first, propagator):
    comps, _, hist_rows, cols = history.shape
    rows = sigma_first.shape[1]
    new_rows = propagator.shape[2]
    blocks = new_rows // rows
    orbitals = comps // 2
    outer = moms // PAIR
    w = rows // CHUNKS
    half = cols // PAIR
    piece = w // outer
    f32, bf16 = jnp.float32, jnp.bfloat16
    dma = pltpu.SemaphoreType.DMA
    vmem = pl.BlockSpec(memory_space=pltpu.VMEM)
    hbm = pl.BlockSpec(memory_space=pl.ANY)
    task = (blocks, CHUNKS, orbitals)
    line = task + (max(outer - 1, 1),)
    green, sigma = pl.pallas_call(
        functools.partial(window_kernel, moms, shards, CHUNKS),
        out_shape=(
            jax.ShapeDtypeStruct((orbitals, 2, rows, cols), f32),
            jax.ShapeDtypeStruct((orbitals, 2, rows, cols), f32),
        ),
        in_specs=[hbm, hbm, vmem],
        out_specs=(vmem, vmem),
        scratch_shapes=[
            pltpu.VMEM((orbitals, 2, hist_rows, cols), f32),
            pltpu.VMEM((orbitals, 2, hist_rows + new_rows, cols), bf16),
            pltpu.VMEM((orbitals, 2, hist_rows + new_rows, cols), bf16),
            pltpu.VMEM((blocks, orbitals, 2, rows, cols), f32),
            pltpu.VMEM(task + (2, w, half), f32),
            pltpu.VMEM((blocks, orbitals, 2, rows, half), f32),
            pltpu.VMEM(line + (2, piece, half), f32),
            pltpu.VMEM((blocks + 1, orbitals, shards, 2, rows, cols), f32),
            pltpu.VMEM((2, w, cols), f32),
            pltpu.VMEM((blocks, comps, rows, 1), f32),
            dma((1 + orbitals,)),
            dma(task), dma(task),
            dma(line), dma(line), dma(line), dma(line),
            dma(task), dma(task),
            dma(task + (shards,)), dma(task + (shards,)),
            dma(task + (shards,)), dma(task + (shards,)),
        ],
        compiler_params=pltpu.CompilerParams(
            collective_id=0, has_side_effects=True, vmem_limit_bytes=56 * 1024 * 1024
        ),
    )(
        history.reshape(orbitals, 2, hist_rows, cols),
        sigma_first.reshape(orbitals, 2, rows, cols),
        propagator,
    )
    green, sigma = pl.pallas_call(
        deliver,
        out_shape=(
            jax.ShapeDtypeStruct((orbitals, 2, rows, cols), f32),
            jax.ShapeDtypeStruct((orbitals, 2, rows, cols), f32),
        ),
        in_specs=[vmem, vmem],
        out_specs=(vmem, vmem),
    )(green, sigma)
    return green.reshape(comps, 1, rows, cols), sigma.reshape(comps, rows, cols)


def body(history, sigma_first, propagator):
    moms, shards = lax.axis_size("mom"), lax.axis_size("tm")
    rows = sigma_first.shape[1]
    tiled = moms % PAIR == 0 and rows % (CHUNKS * (moms // PAIR) * SUBLANES) == 0
    tiled = tiled and shards % PAIR == 0 and history.shape[3] % (PAIR * LANES) == 0
    tiled = tiled and rows % LANES == 0 and history.shape[2] % LANES == 0
    whole = history.shape[2] + propagator.shape[2] == history.shape[3] * shards
    if history.shape[1] == 1 and tiled and whole:
        return kernel_body(moms, shards, history, sigma_first, propagator)
    return plain_body(history, sigma_first, propagator)


def solution(mesh):
    placed = (P(None, "mom", None, "tm"), P(None, None, "tm"), P(None, "mom", None))
    return jax.shard_map(
        body,
        mesh=mesh,
        in_specs=placed,
        out_specs=(P(None, "mom", None, "tm"), P(None, None, "tm")),
        check_vma=False,
    )
```

```python
import functools
import math

import jax
import jax.numpy as jnp
from jax import lax
from jax.experimental import pallas as pl
from jax.experimental.pallas import tpu as pltpu
from jax.sharding import PartitionSpec as P

MESH = pl.DeviceIdType.MESH
PAIR = 2
SUBLANES = 8
LANES = 128
CHUNKS = 2


def contract(sigma, rows):
    parts = []
    for orbital in range(2):
        s_re = sigma[2 * orbital]
        s_im = sigma[2 * orbital + 1]
        h_re = rows[2 * orbital]
        h_im = rows[2 * orbital + 1]
        hp = lax.Precision.HIGHEST
        real_part = jnp.einsum("tu,kus->kts", s_re, h_re, precision=hp) - jnp.einsum(
            "tu,kus->kts", s_im, h_im, precision=hp
        )
        imag_part = jnp.einsum("tu,kus->kts", s_re, h_im, precision=hp) + jnp.einsum(
            "tu,kus->kts", s_im, h_re, precision=hp
        )
        parts.append(real_part)
        parts.append(imag_part)
    return jnp.stack(parts)


def cubic_pair(a_part, b_part):
    return (
        0.1 * (a_part * a_part * a_part - 3.0 * a_part * b_part * b_part),
        0.1 * (3.0 * a_part * a_part * b_part - b_part * b_part * b_part),
    )


def cubic(local):
    return jnp.stack(cubic_pair(local[0], local[1]) + cubic_pair(local[2], local[3]))


def advance(previous, convolved, factor, row_ids, col_ids, step_size):
    inner = previous + step_size * convolved
    parts = []
    for orbital in range(2):
        p_re = factor[2 * orbital][:, :, None]
        p_im = factor[2 * orbital + 1][:, :, None]
        x_re = inner[2 * orbital]
        x_im = inner[2 * orbital + 1]
        parts.append(p_re * x_re - p_im * x_im)
        parts.append(p_re * x_im + p_im * x_re)
    keep = (col_ids[None, :] <= row_ids[:, None]).astype(jnp.float32)
    return jnp.stack(parts) * keep[None, None]


def plain_body(history, sigma_first, propagator):
    local_moms = history.shape[1]
    hist_rows = history.shape[2]
    cols = history.shape[3]
    rows_block = sigma_first.shape[1]
    new_rows = propagator.shape[2]
    blocks = new_rows // rows_block
    time_shards = lax.axis_size("tm")
    mom_shards = lax.axis_size("mom")
    step_size = 1.0 / jnp.sqrt(jnp.float32(cols * time_shards))
    norm_factor = 1.0 / jnp.sqrt(jnp.float32(local_moms * mom_shards))
    col_ids = lax.axis_index("tm") * cols + jnp.arange(cols, dtype=jnp.int32)
    known_ids = jnp.arange(hist_rows, dtype=jnp.int32)
    known = history * (col_ids[None, :] <= known_ids[:, None]).astype(jnp.float32)[None, None]
    buffer = jnp.concatenate(
        [known, jnp.zeros((4, local_moms, new_rows, cols), jnp.float32)], axis=2
    )
    sigma_cols = sigma_first
    green = None
    for block in range(blocks):
        sigma_full = lax.all_gather(sigma_cols, "tm", axis=2, tiled=True)
        start = hist_rows + block * rows_block
        convolved = contract(sigma_full, buffer)
        previous = buffer[:, :, start - rows_block : start, :]
        row_ids = start + jnp.arange(rows_block, dtype=jnp.int32)
        factor = propagator[:, :, block * rows_block : (block + 1) * rows_block]
        green = advance(previous, convolved, factor, row_ids, col_ids, step_size)
        buffer = lax.dynamic_update_slice_in_dim(buffer, green, start, 2)
        local = lax.psum(jnp.sum(green, axis=1), "mom") * norm_factor
        sigma_cols = cubic(local)
    return (green, sigma_cols)


def split(x):
    high = x.astype(jnp.bfloat16)
    return high, (x - high.astype(jnp.float32)).astype(jnp.bfloat16)


def stage_order(blocks, tasks, last_stage):
    lag = (1.5, 2.0, 2.0, 1.5, 1.5, 0.75)
    busy = (1.0, 0.2, 0.2, 0.1, 0.1, 0.1)
    ready = [(0.0, 0, task, 0) for task in range(tasks)]
    now, order = 0.0, []
    while ready:
        item = min(ready)
        ready.remove(item)
        when, block, task, stage = item
        order.append((stage, block, task))
        now = max(now, when) + busy[stage]
        done = now + lag[stage]
        final = block + 1 == blocks
        if stage < last_stage and not (final and stage == 4):
            ready.append((done, block, task, stage + 1))
        elif not final:
            ready.append((done, block + 1, task, 0))
    return order


def window_kernel(
    moms, shards, chunks,
    hist_ref, sig_ref, prop_ref, green_ref, next_ref,
    hist32, gh, gl, gcur, ybuf, part, zbuf, s32, conv, pcol,
    load_sem, ys, yr, zs, zr, gzs, gzr, gys, gyr, ts, tr, fs, fr,
):
    orbitals, _, hist_rows, cols = hist_ref.shape
    rows = sig_ref.shape[2]
    blocks = prop_ref.shape[2] // rows
    outer = moms // PAIR
    w = rows // chunks
    half = cols // PAIR
    piece = w // outer
    dt = 1.0 / math.sqrt(cols * shards)
    norm = 1.0 / math.sqrt(moms)
    mom = lax.axis_index("mom")
    tm = lax.axis_index("tm")
    y = lax.rem(mom, PAIR)
    z = lax.div(mom, PAIR)
    partner = z * PAIR + (1 - y)
    peers = [lax.rem(z + d, outer) * PAIR + y for d in range(1, outer)]
    place = lax.rem(tm, PAIR)
    twin = tm + 1 - 2 * place

    loads = [pltpu.make_async_copy(sig_ref, s32.at[0, :, tm], load_sem.at[0])]
    loads += [
        pltpu.make_async_copy(hist_ref.at[o], hist32.at[o], load_sem.at[1 + o]) for o in range(orbitals)
    ]
    for load in loads:
        load.start()

    barrier = pltpu.get_barrier_semaphore()
    pl.semaphore_signal(barrier, inc=1, device_id=(partner, tm), device_id_type=MESH)
    for peer in peers:
        pl.semaphore_signal(barrier, inc=1, device_id=(peer, tm), device_id_type=MESH)
    for d in range(1, shards):
        pl.semaphore_signal(
            barrier, inc=1, device_id=(mom, lax.rem(tm + d, shards)), device_id_type=MESH
        )
    pl.semaphore_wait(barrier, 1 + len(peers) + shards - 1)

    def width(b, shard):
        return max(0, min(cols, hist_rows + b * rows - shard * cols))

    def remote(src, dst, send, recv, device):
        return pltpu.make_async_remote_copy(
            src_ref=src, dst_ref=dst, send_sem=send, recv_sem=recv,
            device_id=device, device_id_type=MESH,
        )

    def chunk(r):
        return pl.ds(r * w, w)

    def near(b, r, o, src):
        view = s32.at[b, o, src, :, chunk(r), pl.ds(0, width(b, src))]
        return remote(view, view, ts.at[b, r, o, 0], tr.at[b, r, o, src], (mom, jnp.int32(src - 1)))

    def far(b, r, o, src, dst):
        view = s32.at[b, o, src, dst % PAIR, chunk(r), pl.ds(0, width(b, src))]
        return remote(view, view, ts.at[b, r, o, 1 + dst], tr.at[b, r, o, src], (mom, jnp.int32(dst)))

    def passed(b, r, o, src, component):
        view = s32.at[b, o, src, component, chunk(r), pl.ds(0, width(b, src))]
        return remote(view, view, fs.at[b, r, o, src], fr.at[b, r, o, src], (mom, twin))

    def spread(b, r, o, act):
        for src in range(1, shards):
            base = src - src % PAIR
            if width(b, src):
                @pl.when(tm == src)
                def _():
                    for dst in range(base):
                        act(far(b, r, o, src, dst))
                    if src % PAIR:
                        act(near(b, r, o, src))

    def forward(b, r, o, go):
        for src in range(PAIR, shards):
            base = src - src % PAIR
            if width(b, src):
                @pl.when(tm < base)
                def _():
                    if go:
                        far(b, r, o, src, 0).wait_recv()
                        passed(b, r, o, src, place).start()
                    else:
                        passed(b, r, o, src, place).wait_send()

    half_mine = pl.ds(pl.multiple_of(y * half, LANES), half)
    half_other = pl.ds(pl.multiple_of((1 - y) * half, LANES), half)

    def strip(r, k):
        return pl.ds(pl.multiple_of(r * w + k * piece, SUBLANES), piece)

    def pair_sum(b, r, o):
        return remote(
            gcur.at[b, o, :, chunk(r), half_other], ybuf.at[b, r, o],
            ys.at[b, r, o], yr.at[b, r, o], (partner, tm),
        )

    def line_sum(b, r, o, d):
        target = lax.rem(z + d, outer)
        return remote(
            part.at[b, o, :, strip(r, target)], zbuf.at[b, r, o, d - 1],
            zs.at[b, r, o, d - 1], zr.at[b, r, o, d - 1], (peers[d - 1], tm),
        )

    def line_copy(b, r, o, d):
        view = s32.at[b + 1, o, tm, :, strip(r, z), half_mine]
        return remote(view, view, gzs.at[b, r, o, d - 1], gzr.at[b, r, o, d - 1], (peers[d - 1], tm))

    def pair_copy(b, r, o):
        view = s32.at[b + 1, o, tm, :, chunk(r), half_mine]
        return remote(view, view, gys.at[b, r, o], gyr.at[b, r, o], (partner, tm))

    tasks = [(r, o) for r in range(chunks) for o in range(orbitals)]
    start_copy = lambda copy: copy.start()
    loads[0].wait()
    for r, o in tasks:
        spread(0, r, o, start_copy)

    col_ids = tm * cols + lax.broadcasted_iota(jnp.int32, (rows, cols), 1)
    row_iota = lax.broadcasted_iota(jnp.int32, (rows, cols), 0)
    keep_cols = tm * cols + lax.broadcasted_iota(jnp.int32, (w, cols), 1)
    keep_rows = lax.broadcasted_iota(jnp.int32, (w, cols), 0)
    square = lax.broadcasted_iota(jnp.int32, (rows, rows), 0)
    diagonal = square == lax.broadcasted_iota(jnp.int32, (rows, rows), 1)
    for b in range(blocks):
        for c in range(2 * orbitals):
            line = prop_ref[c, :, b * rows : (b + 1) * rows]
            pcol[b, c] = jnp.sum(jnp.where(diagonal, line, 0.0), axis=1, keepdims=True)
    gh[:, :, hist_rows:] = jnp.zeros((orbitals, 2, blocks * rows, cols), jnp.bfloat16)
    gl[:, :, hist_rows:] = jnp.zeros((orbitals, 2, blocks * rows, cols), jnp.bfloat16)
    for o in range(orbitals):
        loads[1 + o].wait()
        for r in range(0, hist_rows, rows):
            for c in range(2):
                x = jnp.where(col_ids <= row_iota + r, hist32[o, c, r : r + rows], 0.0)
                high, low = split(x)
                gh[o, c, r : r + rows] = high
                gl[o, c, r : r + rows] = low
    for r, o in tasks:
        forward(0, r, o, True)

    def compute(b, r, o):
        start = hist_rows + b * rows + r * w
        span = slice(r * w, (r + 1) * w)
        conv[...] = jnp.zeros(conv.shape, jnp.float32)
        for shard in range(shards):
            depth = width(b, shard)
            if not depth:
                continue
            base = shard - shard % PAIR
            if shard % PAIR:
                @pl.when(tm == base)
                def _():
                    near(b, r, o, shard).wait_recv()
            if base:
                @pl.when(tm < base)
                def _():
                    passed(b, r, o, shard, 0).wait_recv()

            @pl.when(tm <= shard)
            def _():
                re_high, re_low = split(s32[b, o, shard, 0, span, 0:depth])
                im_high, im_low = split(s32[b, o, shard, 1, span, 0:depth])
                lhs_high = jnp.concatenate([re_high, im_high], axis=0)
                lhs_both = jnp.concatenate([re_high, im_high, re_low, im_low], axis=0)
                u = shard * cols
                totals = []
                for c in range(2):
                    main = jnp.dot(
                        lhs_both, gh[o, c, u : u + depth], preferred_element_type=jnp.float32
                    )
                    rest = jnp.dot(
                        lhs_high, gl[o, c, u : u + depth], preferred_element_type=jnp.float32
                    )
                    totals.append(main[: 2 * w] + (main[2 * w :] + rest))
                conv[0] += totals[0][:w] - totals[1][w:]
                conv[1] += totals[1][:w] + totals[0][w:]

        p_re = pcol[b, 2 * o, span]
        p_im = pcol[b, 2 * o + 1, span]
        if b == 0:
            before = start - rows
            seen = keep_cols <= keep_rows + before
            prev = [jnp.where(seen, hist32[o, c, before : before + w], 0.0) for c in range(2)]
        else:
            prev = [gcur[b - 1, o, c, span] for c in range(2)]
        x_re = prev[0] + dt * conv[0]
        x_im = prev[1] + dt * conv[1]
        keep = keep_cols <= keep_rows + start
        new = [
            jnp.where(keep, p_re * x_re - p_im * x_im, 0.0),
            jnp.where(keep, p_re * x_im + p_im * x_re, 0.0),
        ]
        for c in range(2):
            gcur[b, o, c, span] = new[c]

        @pl.when(active(b))
        def _():
            pair_sum(b, r, o).start()

        for c in range(2):
            if b + 1 == blocks:
                green_ref[o, c, span] = new[c]
            else:
                high, low = split(new[c])
                gh[o, c, start : start + w] = high
                gl[o, c, start : start + w] = low

    def active(b):
        return tm * cols < hist_rows + (b + 1) * rows

    def sum_pair(b, r, o):
        pair_sum(b, r, o).wait_recv()
        part[b, o, :, chunk(r)] = gcur[b, o, :, chunk(r), half_mine] + ybuf[b, r, o]
        for d in range(1, outer):
            line_sum(b, r, o, d).start()

    def sum_line(b, r, o):
        total = part[b, o, :, strip(r, z)]
        for d in range(1, outer):
            line_sum(b, r, o, d).wait_recv()
            total = total + zbuf[b, r, o, d - 1]
        total = total * norm
        s_re, s_im = cubic_pair(total[0], total[1])
        s32[b + 1, o, tm, 0, strip(r, z), half_mine] = s_re
        s32[b + 1, o, tm, 1, strip(r, z), half_mine] = s_im
        for d in range(1, outer):
            line_copy(b, r, o, d).start()

    def copy_line(b, r, o):
        for d in range(1, outer):
            line_copy(b, r, o, d).wait_recv()
        pair_copy(b, r, o).start()

    def copy_pair(b, r, o):
        pair_copy(b, r, o).wait_recv()
        if b + 1 == blocks:
            next_ref[o, :, chunk(r)] = s32[blocks, o, tm, :, chunk(r)]
        else:
            spread(b + 1, r, o, start_copy)

    stages = (compute, sum_pair, sum_line, copy_line, copy_pair)
    for stage, b, task in stage_order(blocks, len(tasks), 5):
        r, o = tasks[task]
        if stage == 0:
            compute(b, r, o)
        elif stage == 5:
            forward(b + 1, r, o, True)
        else:
            @pl.when(active(b))
            def _():
                stages[stage](b, r, o)

    for b in range(blocks):
        for r, o in tasks:
            spread(b, r, o, lambda copy: copy.wait_send())
            forward(b, r, o, False)

            @pl.when(active(b))
            def _():
                pair_sum(b, r, o).wait_send()
                pair_copy(b, r, o).wait_send()
                for d in range(1, outer):
                    line_sum(b, r, o, d).wait_send()
                    line_copy(b, r, o, d).wait_send()


def deliver(green_ref, sigma_ref, green_out, sigma_out):
    green_out[...] = green_ref[...]
    sigma_out[...] = sigma_ref[...]


def kernel_body(moms, shards, history, sigma_first, propagator):
    comps, _, hist_rows, cols = history.shape
    rows = sigma_first.shape[1]
    new_rows = propagator.shape[2]
    blocks = new_rows // rows
    orbitals = comps // 2
    outer = moms // PAIR
    w = rows // CHUNKS
    half = cols // PAIR
    piece = w // outer
    f32, bf16 = jnp.float32, jnp.bfloat16
    dma = pltpu.SemaphoreType.DMA
    vmem = pl.BlockSpec(memory_space=pltpu.VMEM)
    hbm = pl.BlockSpec(memory_space=pl.ANY)
    task = (blocks, CHUNKS, orbitals)
    line = task + (max(outer - 1, 1),)
    green, sigma = pl.pallas_call(
        functools.partial(window_kernel, moms, shards, CHUNKS),
        out_shape=(
            jax.ShapeDtypeStruct((orbitals, 2, rows, cols), f32),
            jax.ShapeDtypeStruct((orbitals, 2, rows, cols), f32),
        ),
        in_specs=[hbm, hbm, vmem],
        out_specs=(vmem, vmem),
        scratch_shapes=[
            pltpu.VMEM((orbitals, 2, hist_rows, cols), f32),
            pltpu.VMEM((orbitals, 2, hist_rows + new_rows, cols), bf16),
            pltpu.VMEM((orbitals, 2, hist_rows + new_rows, cols), bf16),
            pltpu.VMEM((blocks, orbitals, 2, rows, cols), f32),
            pltpu.VMEM(task + (2, w, half), f32),
            pltpu.VMEM((blocks, orbitals, 2, rows, half), f32),
            pltpu.VMEM(line + (2, piece, half), f32),
            pltpu.VMEM((blocks + 1, orbitals, shards, 2, rows, cols), f32),
            pltpu.VMEM((2, w, cols), f32),
            pltpu.VMEM((blocks, comps, rows, 1), f32),
            dma((1 + orbitals,)),
            dma(task), dma(task),
            dma(line), dma(line), dma(line), dma(line),
            dma(task), dma(task),
            dma(task + (shards,)), dma(task + (shards,)),
            dma(task + (shards,)), dma(task + (shards,)),
        ],
        compiler_params=pltpu.CompilerParams(
            collective_id=0, has_side_effects=True, vmem_limit_bytes=56 * 1024 * 1024
        ),
    )(
        history.reshape(orbitals, 2, hist_rows, cols),
        sigma_first.reshape(orbitals, 2, rows, cols),
        propagator,
    )
    green, sigma = pl.pallas_call(
        deliver,
        out_shape=(
            jax.ShapeDtypeStruct((orbitals, 2, rows, cols), f32),
            jax.ShapeDtypeStruct((orbitals, 2, rows, cols), f32),
        ),
        in_specs=[vmem, vmem],
        out_specs=(vmem, vmem),
    )(green, sigma)
    return green.reshape(comps, 1, rows, cols), sigma.reshape(comps, rows, cols)


def body(history, sigma_first, propagator):
    moms, shards = lax.axis_size("mom"), lax.axis_size("tm")
    rows = sigma_first.shape[1]
    tiled = moms % PAIR == 0 and rows % (CHUNKS * (moms // PAIR) * SUBLANES) == 0
    tiled = tiled and shards % PAIR == 0 and history.shape[3] % (PAIR * LANES) == 0
    tiled = tiled and rows % LANES == 0 and history.shape[2] % LANES == 0
    whole = history.shape[2] + propagator.shape[2] == history.shape[3] * shards
    if history.shape[1] == 1 and tiled and whole:
        return kernel_body(moms, shards, history, sigma_first, propagator)
    return plain_body(history, sigma_first, propagator)


def solution(mesh):
    placed = (P(None, "mom", None, "tm"), P(None, None, "tm"), P(None, "mom", None))
    return jax.shard_map(
        body,
        mesh=mesh,
        in_specs=placed,
        out_specs=(P(None, "mom", None, "tm"), P(None, None, "tm")),
        check_vma=False,
    )
```
